32 devices in a mesh: section: 4 (over z), dp: 2 (over x), tensor: 4 (over y, core).
Axes of the slice: x: 2, y: 2, z: 4, core: 2. Of those that a mesh axis runs over, the one named last changes fastest.
Arguments:
- hidden: bfloat16 [64, 16384], P(('section', 'dp'), 'tensor'), may hold values from -100 to 100
- norm_gain: float32 [16384], replicated, may hold values from 0.5 to 1.5
- head_weight: bfloat16 [8192, 16384], P(('section', 'dp', 'tensor')), may hold values from -100 to 100
- token_ids: int32 [64], P(('section', 'dp')), may hold values from 0 to 8191
- resp_len: int32 [8, 2], P(('section', 'dp')), may hold values from 1 to 4, 6 in all within a row
- group_of: int32 [8, 2], P(('section', 'dp')), may hold values from 0 to 7
- loss_mask: int32 [64], P(('section', 'dp', 'tensor')), may hold values 0 or 1
- old_logp: float32 [64], P(('section', 'dp', 'tensor')), may hold values from -30 to 0
- ref_logp: float32 [64], P(('section', 'dp', 'tensor')), may hold values from -30 to 0
- advantage: float32 [64], P(('section', 'dp', 'tensor')), may hold values from -30 to 30
Outputs:
- token_logp: float32 [64], P(('section', 'dp', 'tensor'))
- group_loss: float32 [8], replicated
- group_count: float32 [8], replicated
The draws below stay inside these ranges and needn't reach their ends.
Inputs may be any that keep to these rules, and one draw needn't show every extreme that they name: `resp_len`: the response lengths of the 2 sequences of each shard sum to exactly 6.
All inputs are finite; a program needn't handle non-finite values. No bound on the sum of `loss_mask` on one device may be relied on, other than what follows from the above.
Results may differ from the reference program's by a relative error of at most 0.0003.
The reference program's roundings to bfloat16 on the way (of `normed`) count: a program that leaves them out, or rounds other values in their place, can miss the bound.
Values may be sent and summed in bfloat16 or wider, within the bound.
No kernel may reach another device: no remote copies, remote signals or barrier semaphores. Data moves between devices by JAX's collectives and lax.ppermute only.
A program may use at most 128 MiB of HBM per device.

```python
import math
import jax
import jax.numpy as jnp
import numpy as np
from jax import lax

D = 16384
V_DEV = 256
VOCAB = 8192
WIN = 4
SEQ_SH = 2
GROUPS = 8
TOK_SH = 8
LIVE = 6
NSH = 8
TOK = 64


def head_row(key, row_id):
    return jax.random.normal(jax.random.fold_in(jax.random.fold_in(key, 7002), row_id), (D,), jnp.float32)


def draw_head_weight(key, part):
    entries = jax.vmap(lambda row_id: head_row(key, row_id))(jnp.arange(VOCAB))
    weights = entries / math.sqrt(D)
    return weights.astype(jnp.bfloat16)


def draw_hidden(key, part):
    values = jax.random.normal(jax.random.fold_in(key, 7003), (TOK, D), jnp.float32)
    values = jnp.clip(values, -6.0, 6.0)
    return values.astype(jnp.bfloat16)


def logp_draw(key, salt):
    spread = jax.random.uniform(jax.random.fold_in(key, salt), (TOK,), jnp.float32, -1.5, 1.5)
    return -math.log(VOCAB) - 0.5 + spread


def draw_old_logp(key, part):
    return logp_draw(key, 7004)


def draw_ref_logp(key, part):
    return logp_draw(key, 7005)


def draw_advantage(key, part):
    slope = jnp.arange(TOK).astype(jnp.float32) / max(TOK - 1, 1)
    values = jnp.clip(jax.random.normal(jax.random.fold_in(key, 7007), (TOK,), jnp.float32), -6.0, 6.0)
    return values * (1.0 + 2.0 * slope)


def touch_ends(drawn, rng, smallest, top_value):
    longest = drawn.shape.index(max(drawn.shape))
    spots = []
    for shift in (0, 1):
        where = [jax.random.randint(jax.random.fold_in(rng, axis), (), 0, length) for axis, length in enumerate(drawn.shape)]
        where[longest] = (where[longest] + shift) % drawn.shape[longest]
        spots.append(tuple(where))
    return drawn.at[spots[0]].set(smallest).at[spots[1]].set(top_value)


def rank_bounds(number_of, lean):
    loads = [(1 << 20) // math.isqrt(grade ** lean) + 1 for grade in range(1, number_of + 1)]
    deviation = 1 + sum(loads) // (1 << 30)
    return np.cumsum(np.array([max(1, weight // deviation) for weight in loads]))


def ranked_ids(key, dims, count, skew):
    listing = rank_bounds(count, skew)
    ticket = jax.random.randint(jax.random.fold_in(key, 1), dims, 0, int(listing[count - 1]))
    rank = jnp.searchsorted(jnp.asarray(listing, jnp.int32), ticket, side="right")
    return jax.random.permutation(jax.random.fold_in(key, 2), count)[rank].astype(jnp.int32)


def split_up(number_of, total, limit, skew):
    loads = [(1 << 20) // math.isqrt(grade ** skew) + 1 for grade in range(2, number_of + 1)]
    spare, counts = total - limit - (number_of - 1), [1] * (number_of - 1)
    while spare > 0:
        movable = [i for i in range(number_of - 1) if counts[i] < limit]
        mass, left = sum([loads[i] for i in movable]), spare
        for i in movable:
            addition = min(limit - counts[i], max(1, left * loads[i] // mass), spare)
            counts[i] = counts[i] + addition
            spare = spare - addition
    return np.array([limit] + counts)


def uneven(rng, number_of, total, limit, skew):
    if number_of == 2:
        one = jax.random.randint(rng, (), max(1, total - limit), min(limit, total - 1) + 1)
        return jnp.stack([one, total - one])
    sizes = jnp.asarray(split_up(number_of, total, limit, skew), jnp.int32)
    couples = (number_of - 1) // 2
    donor, receiver = sizes[1:1 + 2 * couples:2], sizes[2:2 + 2 * couples:2]
    room = jnp.minimum(donor - 1, limit - receiver)
    shifted = jax.random.randint(jax.random.fold_in(rng, 1), (couples,), 0, 1 << 20) % (room + 1)
    sizes = sizes.at[1:1 + 2 * couples:2].set(donor - shifted).at[2:2 + 2 * couples:2].set(receiver + shifted)
    return sizes[jax.random.permutation(jax.random.fold_in(rng, 2), number_of)]


def setup_inputs(seed: int = 0) -> dict:
    seeds = jax.random.split(jax.random.key(seed), 11)
    return {
        "hidden": draw_hidden(jax.random.fold_in(seeds[10], 71), 0),
        "norm_gain": jnp.clip(1.0 + 0.1 * jax.random.normal(seeds[1], (D,), jnp.float32), 0.5, 1.5),
        "head_weight": draw_head_weight(jax.random.fold_in(seeds[10], 71), 0),
        "token_ids": touch_ends(ranked_ids(seeds[3], (TOK,), VOCAB, 2), jax.random.fold_in(seeds[3], 3), 0, VOCAB - 1).astype(jnp.int32),
        "resp_len": jax.vmap(lambda own: uneven(own, SEQ_SH, LIVE, WIN, 0))(jax.random.split(seeds[4], NSH)).reshape((NSH, SEQ_SH)).astype(jnp.int32),
        "group_of": touch_ends(jax.random.randint(seeds[5], (NSH, SEQ_SH), 0, GROUPS), jax.random.fold_in(seeds[5], 1), 0, GROUPS - 1).astype(jnp.int32),
        "loss_mask": touch_ends((jax.random.randint(seeds[6], (TOK,), 0, 4) < 3).astype(jnp.int32), jax.random.fold_in(seeds[6], 1), 0, 1),
        "old_logp": draw_old_logp(jax.random.fold_in(seeds[10], 71), 0),
        "ref_logp": draw_ref_logp(jax.random.fold_in(seeds[10], 71), 0),
        "advantage": draw_advantage(jax.random.fold_in(seeds[10], 71), 0),
    }


epsilon = 1e-05
clip_range = 0.2
kl_weight = 0.1
log_clamp = 20.0

def normalize(hidden, norm_gain):
    values = hidden.astype(jnp.float32)
    mean_square = lax.optimization_barrier(jnp.mean(values * values, axis=1))
    return (values * lax.rsqrt(mean_square + epsilon)[:, None] * norm_gain[None, :]).astype(jnp.bfloat16)

def token_loss(logprob, old_logp, ref_logp, advantage, weight):
    ratios = jnp.exp(logprob - old_logp)
    clipped = jnp.clip(ratios, 1.0 - clip_range, 1.0 + clip_range)
    surrogate = jnp.minimum(ratios * advantage, clipped * advantage)
    log_gap = jnp.clip(ref_logp - logprob, -log_clamp, log_clamp)
    penalty = jnp.exp(log_gap) - log_gap - 1.0
    return (kl_weight * penalty - surrogate) * weight

def reference(hidden, norm_gain, head_weight, token_ids, resp_len, group_of, loss_mask, old_logp, ref_logp, advantage):
    normed = normalize(hidden, norm_gain)
    vocab_block = V_DEV * 32
    block_count = VOCAB // vocab_block
    blocks = head_weight.reshape(block_count, vocab_block, D)
    starts = (jnp.arange(block_count) * vocab_block).astype(jnp.int32)

    def absorb(carried, inputs):
        row_max, totals, chosen = carried
        weights, begin = inputs
        logits = jnp.dot(normed, weights.T, preferred_element_type=jnp.float32)
        column = begin + jnp.arange(vocab_block, dtype=jnp.int32)
        new_max = jnp.maximum(row_max, lax.optimization_barrier(jnp.max(logits, axis=1)))
        totals = totals * jnp.exp(row_max - new_max) + lax.optimization_barrier(jnp.sum(jnp.exp(logits - new_max[:, None]), axis=1))
        chosen = chosen + lax.optimization_barrier(jnp.sum(jnp.where(token_ids[:, None] == column[None, :], logits, 0.0), axis=1))
        return ((new_max, totals, chosen), None)
    initial = (jnp.full((TOK,), -jnp.inf, jnp.float32), jnp.zeros((TOK,), jnp.float32), jnp.zeros((TOK,), jnp.float32))
    (row_max, totals, chosen), unused = lax.scan(absorb, initial, (blocks, starts))
    logprob = chosen - (row_max + jnp.log(totals))
    position = jnp.arange(TOK, dtype=jnp.int32)
    local_row = position % TOK_SH
    seq_flat = position // TOK_SH * SEQ_SH + local_row // WIN
    within = local_row % WIN
    lengths = resp_len.reshape(-1)[seq_flat]
    is_live = within >= WIN - lengths
    token_logp = jnp.where(is_live, logprob, 0.0)
    weight = is_live.astype(jnp.float32) * loss_mask.astype(jnp.float32)
    losses = token_loss(logprob, old_logp, ref_logp, advantage, weight)
    groups = group_of.reshape(-1)[seq_flat]
    member = (groups[:, None] == jnp.arange(GROUPS, dtype=jnp.int32)[None, :]).astype(jnp.float32)
    group_loss = lax.optimization_barrier(jnp.sum(member * losses[:, None], axis=0))
    group_count = lax.optimization_barrier(jnp.sum(member * weight[:, None], axis=0))
    return (token_logp, group_loss, group_count)
```

```python
import jax
import jax.numpy as jnp
from jax import lax
from jax.experimental import pallas as pl
from jax.experimental.pallas import tpu as pltpu
from jax.sharding import PartitionSpec as P

GROUPS = 8
LANES = 128
FIELDS = 6
DIGITS = 3
BASE = 256

epsilon = 1e-05
clip_range = 0.2
kl_weight = 0.1
log_clamp = 20.0

ALL = ("section", "dp", "tensor")


def token_loss(logprob, old_logp, ref_logp, advantage, weight):
    ratios = jnp.exp(logprob - old_logp)
    clipped = jnp.clip(ratios, 1.0 - clip_range, 1.0 + clip_range)
    surrogate = jnp.minimum(ratios * advantage, clipped * advantage)
    log_gap = jnp.clip(ref_logp - logprob, -log_clamp, log_clamp)
    penalty = jnp.exp(log_gap) - log_gap - 1.0
    return (kl_weight * penalty - surrogate) * weight


def spread(x, axis, size, inner=1):
    if size == 1:
        return x
    length = lax.axis_size(axis)
    span = size * inner
    blocks = [x]
    for k in range(1, size):
        pairs = []
        for i in range(length):
            base, rest = i // span * span, i % span
            place, low = rest // inner, rest % inner
            pairs.append((i, base + (place + k) % size * inner + low))
        blocks.append(lax.ppermute(x, axis, pairs))
    return jnp.concatenate(blocks, axis=0)


def head_kernel(sizes, where, *refs):
    rows, half, sections, dps, ys, cores = sizes
    count = 2 * cores
    pieces = refs[:count]
    gain, extra, head, out, weights, normed, sems = refs[count:]
    section, dp, y, core, device = (where[i] for i in range(5))
    vocab = head.shape[0]
    tok = sections * dps * rows
    order = [(c, yr, h) for c in range(cores) for yr in range(ys) for h in range(2)]
    slots = []
    copies = []
    for n, (c, yr, h) in enumerate(order):
        slot = (lax.rem(y + ys - yr, ys) * cores + lax.rem(core + cores - c, cores)) * 2 + h
        slots.append(slot)
        copy = pltpu.make_async_copy(
            head.at[:, pl.ds(pl.multiple_of(slot * half, LANES), half)], weights.at[n], sems.at[n]
        )
        copy.start()
        copies.append(copy)

    def rows_of(n):
        c, yr, h = order[n]
        ref = pieces[c * 2 + h]
        if h == 0:
            size = dps * sections * rows
            return [(0, ref[yr * size : (yr + 1) * size, :half])]
        size = sections * rows
        return [
            (x * size, ref[(x * ys + yr) * size : (x * ys + yr + 1) * size, :half])
            for x in range(dps)
        ]

    def block(n):
        parts = [part for _, part in rows_of(n)]
        return parts[0] if len(parts) == 1 else jnp.concatenate(parts, axis=0)

    total = jnp.zeros((tok, LANES), jnp.float32)
    for n in range(len(order)):
        values = block(n).astype(jnp.float32)
        squares = values * values
        for start in range(0, half, LANES):
            total = total + squares[:, start : start + LANES]
    scale = lax.rsqrt(jnp.sum(total, axis=1, keepdims=True) / (len(order) * half) + epsilon)
    for n in range(len(order)):
        values = block(n).astype(jnp.float32)
        normed[n] = (values * scale * gain[pl.ds(slots[n], 1), :]).astype(jnp.bfloat16)
    logits = jnp.zeros((tok, vocab), jnp.float32)
    for n in range(len(order)):
        copies[n].wait()
        logits = logits + lax.dot_general(
            normed[n], weights[n], (((1,), (1,)), ((), ())), preferred_element_type=jnp.float32
        )
    size = sections * rows
    codes = [
        pieces[1][x * ys * size : x * ys * size + size, half:].astype(jnp.float32) for x in range(dps)
    ]
    codes = codes[0] if dps == 1 else jnp.concatenate(codes, axis=0)
    ids = jnp.zeros((tok, 1), jnp.float32)
    for digit in range(DIGITS):
        ids = ids * BASE + codes[:, digit : digit + 1]
    column = device * vocab + lax.broadcasted_iota(jnp.int32, (tok, vocab), 1)
    row_max = jnp.max(logits, axis=1, keepdims=True)
    sums = jnp.sum(jnp.exp(logits - row_max), axis=1, keepdims=True)
    chosen = jnp.sum(
        jnp.where(ids.astype(jnp.int32) == column, logits, 0.0), axis=1, keepdims=True
    )
    row = lax.broadcasted_iota(jnp.int32, (tok, tok), 0)
    place = lax.broadcasted_iota(jnp.int32, (tok, tok), 1)
    from_x = lax.rem(dp + dps - row // (sections * rows), dps)
    from_z = lax.rem(section + sections - lax.rem(row // rows, sections), sections)
    match = (from_z * dps + from_x) * rows + lax.rem(row, rows) == place
    devices = out.shape[0]
    for n, value in enumerate((row_max, sums, chosen)):
        line = jnp.sum(jnp.where(match, value, 0.0), axis=0, keepdims=True)
        out[:, n * tok : (n + 1) * tok] = jnp.broadcast_to(line, (devices, tok))
    out[:, 3 * tok :] = jnp.broadcast_to(extra[...], (devices, extra.shape[1]))


def loss_kernel(own, where, stats, token_logp, group_loss, group_count):
    devices = stats.shape[0]
    tok = devices * own
    maxima = stats[:, :tok]
    row_max = jnp.max(maxima, axis=0, keepdims=True)
    totals = jnp.sum(stats[:, tok : 2 * tok] * jnp.exp(maxima - row_max), axis=0, keepdims=True)
    chosen = jnp.sum(stats[:, 2 * tok : 3 * tok], axis=0, keepdims=True)
    logprob = chosen - (row_max + jnp.log(totals))
    extra = stats[:, 3 * tok :]
    row = lax.broadcasted_iota(jnp.int32, (devices, tok), 0)
    lane = lax.broadcasted_iota(jnp.int32, (devices, tok), 1)
    mine = lax.broadcasted_iota(jnp.int32, (devices, 1), 0) == where[4]
    group_lane = lax.broadcasted_iota(jnp.int32, (devices, GROUPS), 1).astype(jnp.float32)
    own_lane = lax.broadcasted_iota(jnp.int32, (1, own), 1)
    loss_sum = jnp.zeros((devices, GROUPS), jnp.float32)
    count_sum = jnp.zeros((devices, GROUPS), jnp.float32)
    kept = jnp.zeros((1, own), jnp.float32)
    for j in range(own):
        value = jnp.sum(jnp.where(lane == row * own + j, logprob, 0.0), axis=1, keepdims=True)
        old, ref, advantage, weight, live, group = (
            extra[:, j * FIELDS + f : j * FIELDS + f + 1] for f in range(FIELDS)
        )
        losses = token_loss(value, old, ref, advantage, weight)
        hit = group == group_lane
        loss_sum = loss_sum + jnp.where(hit, losses, 0.0)
        count_sum = count_sum + jnp.where(hit, weight, 0.0)
        result = jnp.sum(jnp.where(mine & (live > 0.0), value, 0.0), axis=0, keepdims=True)
        kept = jnp.where(own_lane == j, result, kept)
    token_logp[...] = kept
    group_loss[...] = jnp.sum(loss_sum, axis=0, keepdims=True)
    group_count[...] = jnp.sum(count_sum, axis=0, keepdims=True)


def local(
    hidden,
    norm_gain,
    head_weight,
    token_ids,
    resp_len,
    group_of,
    loss_mask,
    old_logp,
    ref_logp,
    advantage,
):
    rows, width = hidden.shape
    half = width // 2
    sections, dps, tensors = (lax.axis_size(a) for a in ALL)
    devices = sections * dps * tensors
    cores = 2 if tensors % 2 == 0 else 1
    ys = tensors // cores
    tensor_idx = lax.axis_index("tensor")
    device = lax.axis_index(ALL)
    own = loss_mask.shape[0]

    seq_count = resp_len.shape[1]
    window = rows // seq_count
    own_row = tensor_idx * own + jnp.arange(own, dtype=jnp.int32)
    member = (own_row // window)[:, None] == jnp.arange(seq_count, dtype=jnp.int32)[None, :]
    length = jnp.sum(jnp.where(member, resp_len, 0), axis=1)
    group = jnp.sum(jnp.where(member, group_of, 0), axis=1)
    live = (own_row % window >= window - length).astype(jnp.float32)
    weight = live * loss_mask.astype(jnp.float32)
    fields = jnp.stack(
        [old_logp, ref_logp, advantage, weight, live, group.astype(jnp.float32)], axis=1
    ).reshape(1, own * FIELDS)
    extra_width = -(-own * FIELDS // LANES) * LANES
    extra = jnp.pad(fields, ((0, 0), (0, extra_width - own * FIELDS)))

    digits = jnp.stack(
        [token_ids // BASE ** (DIGITS - 1 - d) % BASE for d in range(DIGITS)], axis=1
    ).astype(jnp.bfloat16)
    codes = jnp.pad(digits, ((0, 0), (0, LANES - DIGITS)))

    first = hidden[:, :half]
    second = jnp.concatenate([hidden[:, half:], codes], axis=1)
    first = spread(first, "section", sections)
    second = spread(second, "section", sections)
    first = spread(first, "dp", dps)
    second = spread(second, "tensor", ys, cores)
    first = spread(first, "tensor", ys, cores)
    second = spread(second, "dp", dps)
    pieces = [first, second]
    for k in range(1, cores):
        pairs = [(i, i // cores * cores + (i + k) % cores) for i in range(tensors)]
        pieces += [lax.ppermute(first, "tensor", pairs), lax.ppermute(second, "tensor", pairs)]

    where = jnp.stack(
        [
            lax.axis_index("section"),
            lax.axis_index("dp"),
            tensor_idx // cores,
            tensor_idx % cores,
            device,
        ]
    ).astype(jnp.int32)
    tok = sections * dps * rows
    blocks = 2 * tensors
    vocab = head_weight.shape[0]
    vmem = pl.BlockSpec(memory_space=pltpu.VMEM)
    smem = pl.BlockSpec(memory_space=pltpu.SMEM)
    stats = pl.pallas_call(
        lambda *refs: head_kernel((rows, half, sections, dps, ys, cores), *refs),
        out_shape=jax.ShapeDtypeStruct((devices, 3 * tok + extra_width), jnp.float32),
        in_specs=[smem] + [vmem] * (len(pieces) + 2) + [pl.BlockSpec(memory_space=pl.ANY)],
        out_specs=vmem,
        scratch_shapes=[
            pltpu.VMEM((blocks, vocab, half), jnp.bfloat16),
            pltpu.VMEM((blocks, tok, half), jnp.bfloat16),
            pltpu.SemaphoreType.DMA((blocks,)),
        ],
    )(where, *pieces, norm_gain.reshape(blocks, half), extra, head_weight)
    stats = lax.all_to_all(stats, ALL, 0, 0, tiled=True)
    token_logp, group_loss, group_count = pl.pallas_call(
        lambda *refs: loss_kernel(own, *refs),
        out_shape=[
            jax.ShapeDtypeStruct((1, own), jnp.float32),
            jax.ShapeDtypeStruct((1, GROUPS), jnp.float32),
            jax.ShapeDtypeStruct((1, GROUPS), jnp.float32),
        ],
        in_specs=[smem, vmem],
        out_specs=[vmem] * 3,
    )(where, stats)
    return (token_logp[0], group_loss[0], group_count[0])


def solution(mesh):
    return jax.shard_map(
        local,
        mesh=mesh,
        in_specs=(
            P(("section", "dp"), "tensor"),
            P(),
            P(("section", "dp", "tensor"), None),
            P(("section", "dp")),
            P(("section", "dp"), None),
            P(("section", "dp"), None),
            P(("section", "dp", "tensor")),
            P(("section", "dp", "tensor")),
            P(("section", "dp", "tensor")),
            P(("section", "dp", "tensor")),
        ),
        out_specs=(P(("section", "dp", "tensor")), P(), P()),
        check_vma=False,
    )
```

```python
import jax
import jax.numpy as jnp
from jax import lax
from jax.experimental import pallas as pl
from jax.experimental.pallas import tpu as pltpu
from jax.sharding import PartitionSpec as P

GROUPS = 8
LANES = 128
FIELDS = 6
DIGITS = 3
BITS = 8

epsilon = 1e-05
clip_range = 0.2
kl_weight = 0.1
log_clamp = 20.0

ALL = ("section", "dp", "tensor")


def token_loss(logprob, old_logp, ref_logp, advantage, weight):
    ratios = jnp.exp(logprob - old_logp)
    clipped = jnp.clip(ratios, 1.0 - clip_range, 1.0 + clip_range)
    surrogate = jnp.minimum(ratios * advantage, clipped * advantage)
    log_gap = jnp.clip(ref_logp - logprob, -log_clamp, log_clamp)
    penalty = jnp.exp(log_gap) - log_gap - 1.0
    return (kl_weight * penalty - surrogate) * weight


def spread(x, axis, size, inner=1):
    if size == 1:
        return x
    length = lax.axis_size(axis)
    span = size * inner
    blocks = [x]
    for k in range(1, size):
        pairs = []
        for i in range(length):
            base, rest = i // span * span, i % span
            place, low = rest // inner, rest % inner
            pairs.append((i, base + (place + k) % size * inner + low))
        blocks.append(lax.ppermute(x, axis, pairs))
    return jnp.concatenate(blocks, axis=0)


def head_kernel(sizes, where, *refs):
    rows, half, sections, dps, ys, cores = sizes
    count = 2 * cores
    pieces = refs[:count]
    gain, extra, head, out, weights, normed, sems = refs[count:]
    section, dp, y, core, device = (where[i] for i in range(5))
    vocab = head.shape[0]
    tok = sections * dps * rows
    order = [(c, yr, h) for c in range(cores) for yr in range(ys) for h in range(2)]
    slots = []
    copies = []
    for n, (c, yr, h) in enumerate(order):
        slot = (lax.rem(y + ys - yr, ys) * cores + lax.rem(core + cores - c, cores)) * 2 + h
        slots.append(slot)
        copy = pltpu.make_async_copy(
            head.at[:, pl.ds(pl.multiple_of(slot * half, LANES), half)], weights.at[n], sems.at[n]
        )
        copy.start()
        copies.append(copy)

    def rows_of(n):
        c, yr, h = order[n]
        ref = pieces[c * 2 + h]
        if h == 0:
            size = dps * sections * rows
            return [(0, ref[yr * size : (yr + 1) * size, :half])]
        size = sections * rows
        return [
            (x * size, ref[(x * ys + yr) * size : (x * ys + yr + 1) * size, :half])
            for x in range(dps)
        ]

    def block(n):
        parts = [part for _, part in rows_of(n)]
        return parts[0] if len(parts) == 1 else jnp.concatenate(parts, axis=0)

    total = jnp.zeros((tok, LANES), jnp.float32)
    for n in range(len(order)):
        values = block(n).astype(jnp.float32)
        squares = values * values
        for start in range(0, half, LANES):
            total = total + squares[:, start : start + LANES]
    scale = lax.rsqrt(jnp.sum(total, axis=1, keepdims=True) / (len(order) * half) + epsilon)
    for n in range(len(order)):
        values = block(n).astype(jnp.float32)
        normed[n] = (values * scale * gain[pl.ds(slots[n], 1), :]).astype(jnp.bfloat16)
    logits = jnp.zeros((tok, vocab), jnp.float32)
    for n in range(len(order)):
        copies[n].wait()
        logits = logits + lax.dot_general(
            normed[n], weights[n], (((1,), (1,)), ((), ())), preferred_element_type=jnp.float32
        )
    size = sections * rows
    codes = [
        pieces[1][x * ys * size : x * ys * size + size, half:].astype(jnp.float32) for x in range(dps)
    ]
    codes = codes[0] if dps == 1 else jnp.concatenate(codes, axis=0)
    ids = jnp.zeros((tok, 1), jnp.float32)
    for digit in range(DIGITS):
        ids = ids * 2**BITS + codes[:, digit : digit + 1]
    column = device * vocab + lax.broadcasted_iota(jnp.int32, (tok, vocab), 1)
    row_max = jnp.max(logits, axis=1, keepdims=True)
    sums = jnp.sum(jnp.exp(logits - row_max), axis=1, keepdims=True)
    chosen = jnp.sum(
        jnp.where(ids.astype(jnp.int32) == column, logits, 0.0), axis=1, keepdims=True
    )
    row = lax.broadcasted_iota(jnp.int32, (tok, tok), 0)
    place = lax.broadcasted_iota(jnp.int32, (tok, tok), 1)
    from_x = lax.rem(dp + dps - row // (sections * rows), dps)
    from_z = lax.rem(section + sections - lax.rem(row // rows, sections), sections)
    match = (from_z * dps + from_x) * rows + lax.rem(row, rows) == place
    lines = []
    for n, value in enumerate((row_max, sums, chosen)):
        line = jnp.sum(jnp.where(match, value, 0.0), axis=0, keepdims=True)
        lines.append(line)
    line = jnp.concatenate(lines + [extra[...]], axis=1)
    out[...] = jnp.broadcast_to(line[None], out.shape)


def loss_kernel(own, where, stats, token_logp, group_loss, group_count):
    devices = stats.shape[0]
    tok = devices * own
    stats = stats[:, 0, :]
    maxima = stats[:, :tok]
    row_max = jnp.max(maxima, axis=0, keepdims=True)
    totals = jnp.sum(stats[:, tok : 2 * tok] * jnp.exp(maxima - row_max), axis=0, keepdims=True)
    chosen = jnp.sum(stats[:, 2 * tok : 3 * tok], axis=0, keepdims=True)
    logprob = chosen - (row_max + jnp.log(totals))
    extra = stats[:, 3 * tok :]
    row = lax.broadcasted_iota(jnp.int32, (devices, tok), 0)
    lane = lax.broadcasted_iota(jnp.int32, (devices, tok), 1)
    mine = lax.broadcasted_iota(jnp.int32, (devices, 1), 0) == where[4]
    group_lane = lax.broadcasted_iota(jnp.int32, (devices, GROUPS), 1).astype(jnp.float32)
    own_lane = lax.broadcasted_iota(jnp.int32, (1, own), 1)
    loss_sum = jnp.zeros((devices, GROUPS), jnp.float32)
    count_sum = jnp.zeros((devices, GROUPS), jnp.float32)
    kept = jnp.zeros((1, own), jnp.float32)
    for j in range(own):
        value = jnp.sum(jnp.where(lane == row * own + j, logprob, 0.0), axis=1, keepdims=True)
        old, ref, advantage, weight, live, group = (
            extra[:, f * own + j : f * own + j + 1] for f in range(FIELDS)
        )
        losses = token_loss(value, old, ref, advantage, weight)
        hit = group == group_lane
        loss_sum = loss_sum + jnp.where(hit, losses, 0.0)
        count_sum = count_sum + jnp.where(hit, weight, 0.0)
        result = jnp.sum(jnp.where(mine & (live > 0.0), value, 0.0), axis=0, keepdims=True)
        kept = jnp.where(own_lane == j, result, kept)
    token_logp[...] = kept
    group_loss[...] = jnp.sum(loss_sum, axis=0, keepdims=True)
    group_count[...] = jnp.sum(count_sum, axis=0, keepdims=True)


def local(
    hidden,
    norm_gain,
    head_weight,
    token_ids,
    resp_len,
    group_of,
    loss_mask,
    old_logp,
    ref_logp,
    advantage,
):
    rows, width = hidden.shape
    half = width // 2
    sections, dps, tensors = (lax.axis_size(a) for a in ALL)
    devices = sections * dps * tensors
    cores = 2 if tensors % 2 == 0 else 1
    ys = tensors // cores
    tensor_idx = lax.axis_index("tensor")
    device = lax.axis_index(ALL)
    own = loss_mask.shape[0]

    seq_count = resp_len.shape[1]
    window = rows // seq_count
    own_row = tensor_idx * own + jnp.arange(own, dtype=jnp.int32)
    member = (own_row // window)[:, None] == jnp.arange(seq_count, dtype=jnp.int32)[None, :]
    length = jnp.sum(jnp.where(member, resp_len, 0), axis=1)
    group = jnp.sum(jnp.where(member, group_of, 0), axis=1)
    live = (own_row % window >= window - length).astype(jnp.float32)
    weight = live * loss_mask.astype(jnp.float32)
    extra_width = -(-own * FIELDS // LANES) * LANES
    unused = jnp.zeros((extra_width - own * FIELDS,), jnp.float32)
    extra = jnp.concatenate(
        [old_logp, ref_logp, advantage, weight, live, group.astype(jnp.float32), unused]
    )[None, :]

    digit = jnp.arange(LANES, dtype=jnp.int32)[None, :]
    shift = BITS * jnp.maximum(DIGITS - 1 - digit, 0)
    codes = lax.shift_right_logical(
        jnp.broadcast_to(token_ids[:, None], (rows, LANES)), jnp.broadcast_to(shift, (rows, LANES))
    )
    codes = jnp.where(digit < DIGITS, codes & (2**BITS - 1), 0).astype(jnp.bfloat16)

    column = spread(jnp.concatenate([hidden, codes], axis=1), "section", sections)
    first, second = column[:, :half], column[:, half:]
    first = spread(first, "dp", dps)
    second = spread(second, "tensor", ys, cores)
    first = spread(first, "tensor", ys, cores)
    second = spread(second, "dp", dps)
    where = jnp.stack(
        [
            lax.axis_index("section"),
            lax.axis_index("dp"),
            tensor_idx // cores,
            tensor_idx % cores,
            device,
        ]
    ).astype(jnp.int32)
    blocks = 2 * tensors
    gain = norm_gain.reshape(blocks, half)
    second, gain, extra, where = lax.optimization_barrier((second, gain, extra, where))
    pieces = [first, second]
    for k in range(1, cores):
        pairs = [(i, i // cores * cores + (i + k) % cores) for i in range(tensors)]
        pieces += [lax.ppermute(first, "tensor", pairs), lax.ppermute(second, "tensor", pairs)]

    tok = sections * dps * rows
    vocab = head_weight.shape[0]
    vmem = pl.BlockSpec(memory_space=pltpu.VMEM)
    smem = pl.BlockSpec(memory_space=pltpu.SMEM)
    stats = pl.pallas_call(
        lambda *refs: head_kernel((rows, half, sections, dps, ys, cores), *refs),
        out_shape=jax.ShapeDtypeStruct((devices, 1, 3 * tok + extra_width), jnp.float32),
        in_specs=[smem] + [vmem] * (len(pieces) + 2) + [pl.BlockSpec(memory_space=pl.ANY)],
        out_specs=vmem,
        scratch_shapes=[
            pltpu.VMEM((blocks, vocab, half), jnp.bfloat16),
            pltpu.VMEM((blocks, tok, half), jnp.bfloat16),
            pltpu.SemaphoreType.DMA((blocks,)),
        ],
    )(where, *pieces, gain, extra, head_weight)
    stats = lax.all_to_all(stats, ALL, 0, 0)
    token_logp, group_loss, group_count = pl.pallas_call(
        lambda *refs: loss_kernel(own, *refs),
        out_shape=[
            jax.ShapeDtypeStruct((1, own), jnp.float32),
            jax.ShapeDtypeStruct((1, GROUPS), jnp.float32),
            jax.ShapeDtypeStruct((1, GROUPS), jnp.float32),
        ],
        in_specs=[smem, vmem],
        out_specs=[vmem] * 3,
    )(where, stats)
    return (token_logp[0], group_loss[0], group_count[0])


def solution(mesh):
    return jax.shard_map(
        local,
        mesh=mesh,
        in_specs=(
            P(("section", "dp"), "tensor"),
            P(),
            P(("section", "dp", "tensor"), None),
            P(("section", "dp")),
            P(("section", "dp"), None),
            P(("section", "dp"), None),
            P(("section", "dp", "tensor")),
            P(("section", "dp", "tensor")),
            P(("section", "dp", "tensor")),
            P(("section", "dp", "tensor")),
        ),
        out_specs=(P(("section", "dp", "tensor")), P(), P()),
        check_vma=False,
    )
```

```python
import jax
import jax.numpy as jnp
from jax import lax
from jax.experimental import pallas as pl
from jax.experimental.pallas import tpu as pltpu
from jax.sharding import PartitionSpec as P

GROUPS = 8
LANES = 128
FIELDS = 6
DIGITS = 3
BITS = 8
VMEM_BYTES = 2**22

epsilon = 1e-05
clip_range = 0.2
kl_weight = 0.1
log_clamp = 20.0

ALL = ("section", "dp", "tensor")


def token_loss(logprob, old_logp, ref_logp, advantage, weight):
    ratios = jnp.exp(logprob - old_logp)
    clipped = jnp.clip(ratios, 1.0 - clip_range, 1.0 + clip_range)
    surrogate = jnp.minimum(ratios * advantage, clipped * advantage)
    log_gap = jnp.clip(ref_logp - logprob, -log_clamp, log_clamp)
    penalty = jnp.exp(log_gap) - log_gap - 1.0
    return (kl_weight * penalty - surrogate) * weight


def spread(x, axis, size, inner=1):
    if size == 1:
        return x
    length = lax.axis_size(axis)
    span = size * inner
    blocks = [x]
    for k in range(1, size):
        pairs = []
        for i in range(length):
            base, rest = i // span * span, i % span
            place, low = rest // inner, rest % inner
            pairs.append((i, base + (place + k) % size * inner + low))
        blocks.append(lax.ppermute(x, axis, pairs))
    return jnp.concatenate(blocks, axis=0)


def head_kernel(sizes, where, *refs):
    rows, half, sections, dps, ys, cores = sizes
    count = 2 * cores
    pieces = refs[:count]
    gain, extra, head, out, weights, normed, sems = refs[count:]
    section, dp, y, core, device = (where[i] for i in range(5))
    vocab = head.shape[0]
    tok = sections * dps * rows
    order = [(c, yr, h) for c in range(cores) for yr in range(ys) for h in range(2)]
    slots = []
    copies = []
    for n, (c, yr, h) in enumerate(order):
        slot = (lax.rem(y + ys - yr, ys) * cores + lax.rem(core + cores - c, cores)) * 2 + h
        slots.append(slot)
        copy = pltpu.make_async_copy(
            head.at[:, pl.ds(pl.multiple_of(slot * half, LANES), half)], weights.at[n], sems.at[n]
        )
        copy.start()
        copies.append(copy)

    def rows_of(n):
        c, yr, h = order[n]
        ref = pieces[c * 2 + h]
        if h == 0:
            size = dps * sections * rows
            return [(0, ref[yr * size : (yr + 1) * size, :half])]
        size = sections * rows
        return [
            (x * size, ref[(x * ys + yr) * size : (x * ys + yr + 1) * size, :half])
            for x in range(dps)
        ]

    def block(n):
        parts = [part for _, part in rows_of(n)]
        return parts[0] if len(parts) == 1 else jnp.concatenate(parts, axis=0)

    total = jnp.zeros((tok, LANES), jnp.float32)
    for n in range(len(order)):
        values = block(n).astype(jnp.float32)
        squares = values * values
        for start in range(0, half, LANES):
            total = total + squares[:, start : start + LANES]
    scale = lax.rsqrt(jnp.sum(total, axis=1, keepdims=True) / (len(order) * half) + epsilon)
    for n in range(len(order)):
        values = block(n).astype(jnp.float32)
        normed[n] = (values * scale * gain[pl.ds(slots[n], 1), :]).astype(jnp.bfloat16)
    logits = jnp.zeros((tok, vocab), jnp.float32)
    for n in range(len(order)):
        copies[n].wait()
        logits = logits + lax.dot_general(
            normed[n], weights[n], (((1,), (1,)), ((), ())), preferred_element_type=jnp.float32
        )
    size = sections * rows
    codes = [
        pieces[1][x * ys * size : x * ys * size + size, half:].astype(jnp.float32) for x in range(dps)
    ]
    codes = codes[0] if dps == 1 else jnp.concatenate(codes, axis=0)
    ids = jnp.zeros((tok, 1), jnp.float32)
    for digit in range(DIGITS):
        ids = ids * 2**BITS + codes[:, digit : digit + 1]
    column = device * vocab + lax.broadcasted_iota(jnp.int32, (tok, vocab), 1)
    row_max = jnp.max(logits, axis=1, keepdims=True)
    sums = jnp.sum(jnp.exp(logits - row_max), axis=1, keepdims=True)
    chosen = jnp.sum(
        jnp.where(ids.astype(jnp.int32) == column, logits, 0.0), axis=1, keepdims=True
    )
    row = lax.broadcasted_iota(jnp.int32, (tok, tok), 0)
    place = lax.broadcasted_iota(jnp.int32, (tok, tok), 1)
    from_x = lax.rem(dp + dps - row // (sections * rows), dps)
    from_z = lax.rem(section + sections - lax.rem(row // rows, sections), sections)
    match = (from_z * dps + from_x) * rows + lax.rem(row, rows) == place
    lines = []
    for n, value in enumerate((row_max, sums, chosen)):
        line = jnp.sum(jnp.where(match, value, 0.0), axis=0, keepdims=True)
        lines.append(line)
    line = jnp.concatenate(lines + [extra[...]], axis=1)
    out[...] = jnp.broadcast_to(line[None], out.shape)


def loss_kernel(own, where, stats, token_logp, group_loss, group_count):
    devices = stats.shape[0]
    tok = devices * own
    stats = stats[:, 0, :]
    maxima = stats[:, :tok]
    row_max = jnp.max(maxima, axis=0, keepdims=True)
    totals = jnp.sum(stats[:, tok : 2 * tok] * jnp.exp(maxima - row_max), axis=0, keepdims=True)
    chosen = jnp.sum(stats[:, 2 * tok : 3 * tok], axis=0, keepdims=True)
    logprob = chosen - (row_max + jnp.log(totals))
    extra = stats[:, 3 * tok :]
    row = lax.broadcasted_iota(jnp.int32, (devices, tok), 0)
    lane = lax.broadcasted_iota(jnp.int32, (devices, tok), 1)
    mine = lax.broadcasted_iota(jnp.int32, (devices, 1), 0) == where[4]
    group_lane = lax.broadcasted_iota(jnp.int32, (devices, GROUPS), 1).astype(jnp.float32)
    own_lane = lax.broadcasted_iota(jnp.int32, (1, own), 1)
    loss_sum = jnp.zeros((devices, GROUPS), jnp.float32)
    count_sum = jnp.zeros((devices, GROUPS), jnp.float32)
    kept = jnp.zeros((1, own), jnp.float32)
    for j in range(own):
        value = jnp.sum(jnp.where(lane == row * own + j, logprob, 0.0), axis=1, keepdims=True)
        old, ref, advantage, weight, live, group = (
            extra[:, f * own + j : f * own + j + 1] for f in range(FIELDS)
        )
        losses = token_loss(value, old, ref, advantage, weight)
        hit = group == group_lane
        loss_sum = loss_sum + jnp.where(hit, losses, 0.0)
        count_sum = count_sum + jnp.where(hit, weight, 0.0)
        result = jnp.sum(jnp.where(mine & (live > 0.0), value, 0.0), axis=0, keepdims=True)
        kept = jnp.where(own_lane == j, result, kept)
    token_logp[...] = kept
    group_loss[...] = jnp.sum(loss_sum, axis=0, keepdims=True)
    group_count[...] = jnp.sum(count_sum, axis=0, keepdims=True)


def local(
    hidden,
    norm_gain,
    head_weight,
    token_ids,
    resp_len,
    group_of,
    loss_mask,
    old_logp,
    ref_logp,
    advantage,
):
    rows, width = hidden.shape
    half = width // 2
    sections, dps, tensors = (lax.axis_size(a) for a in ALL)
    devices = sections * dps * tensors
    cores = 2 if tensors % 2 == 0 else 1
    ys = tensors // cores
    tensor_idx = lax.axis_index("tensor")
    device = lax.axis_index(ALL)
    own = loss_mask.shape[0]

    seq_count = resp_len.shape[1]
    window = rows // seq_count
    own_row = tensor_idx * own + jnp.arange(own, dtype=jnp.int32)
    member = (own_row // window)[:, None] == jnp.arange(seq_count, dtype=jnp.int32)[None, :]
    length = jnp.sum(jnp.where(member, resp_len, 0), axis=1)
    group = jnp.sum(jnp.where(member, group_of, 0), axis=1)
    live = (own_row % window >= window - length).astype(jnp.float32)
    weight = live * loss_mask.astype(jnp.float32)
    extra_width = -(-own * FIELDS // LANES) * LANES
    unused = jnp.zeros((extra_width - own * FIELDS,), jnp.float32)
    extra = jnp.concatenate(
        [old_logp, ref_logp, advantage, weight, live, group.astype(jnp.float32), unused]
    )[None, :]

    digit = jnp.arange(LANES, dtype=jnp.int32)[None, :]
    shift = BITS * jnp.maximum(DIGITS - 1 - digit, 0)
    codes = lax.shift_right_logical(
        jnp.broadcast_to(token_ids[:, None], (rows, LANES)), jnp.broadcast_to(shift, (rows, LANES))
    )
    codes = jnp.where(digit < DIGITS, codes & (2**BITS - 1), 0).astype(jnp.bfloat16)

    column = spread(jnp.concatenate([hidden, codes], axis=1), "section", sections)
    first, second = column[:, :half], column[:, half:]
    first = spread(first, "dp", dps)
    second = spread(second, "tensor", ys, cores)
    first = spread(first, "tensor", ys, cores)
    second = spread(second, "dp", dps)
    where = jnp.stack(
        [
            lax.axis_index("section"),
            lax.axis_index("dp"),
            tensor_idx // cores,
            tensor_idx % cores,
            device,
        ]
    ).astype(jnp.int32)
    blocks = 2 * tensors
    gain = norm_gain.reshape(blocks, half)
    second, gain, extra, where = lax.optimization_barrier((second, gain, extra, where))
    pieces = [first, second]
    for k in range(1, cores):
        pairs = [(i, i // cores * cores + (i + k) % cores) for i in range(tensors)]
        pieces += [lax.ppermute(first, "tensor", pairs), lax.ppermute(second, "tensor", pairs)]

    tok = sections * dps * rows
    vocab = head_weight.shape[0]
    vmem = pl.BlockSpec(memory_space=pltpu.VMEM)
    smem = pl.BlockSpec(memory_space=pltpu.SMEM)
    if sum(piece.size * piece.dtype.itemsize for piece in pieces) <= VMEM_BYTES:
        pieces = [pltpu.with_memory_space_constraint(piece, pltpu.VMEM) for piece in pieces]
    stats = pl.pallas_call(
        lambda *refs: head_kernel((rows, half, sections, dps, ys, cores), *refs),
        out_shape=jax.ShapeDtypeStruct((devices, 1, 3 * tok + extra_width), jnp.float32),
        in_specs=[smem] + [vmem] * (len(pieces) + 2) + [pl.BlockSpec(memory_space=pl.ANY)],
        out_specs=vmem,
        scratch_shapes=[
            pltpu.VMEM((blocks, vocab, half), jnp.bfloat16),
            pltpu.VMEM((blocks, tok, half), jnp.bfloat16),
            pltpu.SemaphoreType.DMA((blocks,)),
        ],
    )(where, *pieces, gain, extra, head_weight)
    stats = lax.all_to_all(stats, ALL, 0, 0)
    token_logp, group_loss, group_count = pl.pallas_call(
        lambda *refs: loss_kernel(own, *refs),
        out_shape=[
            jax.ShapeDtypeStruct((1, own), jnp.float32),
            jax.ShapeDtypeStruct((1, GROUPS), jnp.float32),
            jax.ShapeDtypeStruct((1, GROUPS), jnp.float32),
        ],
        in_specs=[smem, vmem],
        out_specs=[vmem] * 3,
    )(where, stats)
    return (token_logp[0], group_loss[0], group_count[0])


def solution(mesh):
    return jax.shard_map(
        local,
        mesh=mesh,
        in_specs=(
            P(("section", "dp"), "tensor"),
            P(),
            P(("section", "dp", "tensor"), None),
            P(("section", "dp")),
            P(("section", "dp"), None),
            P(("section", "dp"), None),
            P(("section", "dp", "tensor")),
            P(("section", "dp", "tensor")),
            P(("section", "dp", "tensor")),
            P(("section", "dp", "tensor")),
        ),
        out_specs=(P(("section", "dp", "tensor")), P(), P()),
        check_vma=False,
    )
```
